32 devices in a mesh: grp: 8 (over z, core), col: 4 (over y, x).
Axes of the slice: x: 2, y: 2, z: 4, core: 2. Of those that a mesh axis runs over, the one named last changes fastest.
Arguments:
- constraint_rows: float32 [2048, 16384], P('grp', 'col'), may hold values from -0.1875 to 0.1875
- shift: float32 [16384], P('col'), may hold values from 0.3 to 1
- group_rows: int32 [8], replicated, may hold values from 1 to 256, 1024 in all
- panel_index: int32 [1], replicated, may hold values from 0 to 31
Outputs:
- panel_factor: float32 [16384, 512], P(('col', 'grp'))
The draws below stay inside these ranges and needn't reach their ends.
Inputs may be any that keep to these rules, and one draw needn't show every extreme that they name: `group_rows`: the values sum to 1024 and the largest equals 256.
All inputs are finite; a program needn't handle non-finite values.
Results may differ from the reference program's by a relative error of at most 0.000076.
Values sent between devices are 32-bit elements; how exact they have to be, the bound alone decides.
No kernel may reach another device: no remote copies, remote signals or barrier semaphores. Data moves between devices by JAX's collectives and lax.ppermute only.
A program may use at most 64 MiB of HBM per device.

```python
import math
import jax
import jax.numpy as jnp
import numpy as np
from jax import lax

NQ = 16384
PANEL = 512
GROUP_ROWS = 256
ALL_ROWS = 2048
N_GRP = 8


def shard_levels(key, shape, shards, smallest, top_value):
    level, own = 1.0, jax.random.fold_in(key, 6)
    for axis_at, blocks in shards:
        heights = jnp.exp(jax.random.uniform(jax.random.fold_in(own, axis_at), (blocks,), jnp.float32, smallest / len(shards), top_value / len(shards)))
        level = level * jnp.repeat(heights, shape[axis_at] // blocks).reshape([-1 if axis == axis_at else 1 for axis in range(len(shape))])
    return level


def profile(count, total, reach, skew):
    portions = [(1 << 20) // math.isqrt(grade ** skew) + 1 for grade in range(2, count + 1)]
    surplus, holding = total - reach - (count - 1), [1] * (count - 1)
    while surplus > 0:
        movable = [i for i in range(count - 1) if holding[i] < reach]
        pool, left = sum([portions[i] for i in movable]), surplus
        for i in movable:
            addition = min(reach - holding[i], max(1, left * portions[i] // pool), surplus)
            holding[i] = holding[i] + addition
            surplus = surplus - addition
    return np.array([reach] + holding)


def ragged(own_key, number_of, total, reach, lean):
    if number_of == 2:
        one = jax.random.randint(own_key, (), max(1, total - reach), min(reach, total - 1) + 1)
        return jnp.stack([one, total - one])
    tallies = jnp.asarray(profile(number_of, total, reach, lean), jnp.int32)
    pairs = (number_of - 1) // 2
    source_of, taker = tallies[1:1 + 2 * pairs:2], tallies[2:2 + 2 * pairs:2]
    slack = jnp.minimum(source_of - 1, reach - taker)
    shifted = jax.random.randint(jax.random.fold_in(own_key, 1), (pairs,), 0, 1 << 20) % (slack + 1)
    tallies = tallies.at[1:1 + 2 * pairs:2].set(source_of - shifted).at[2:2 + 2 * pairs:2].set(taker + shifted)
    return tallies[jax.random.permutation(jax.random.fold_in(own_key, 2), number_of)]


def gaussian(stream_key, shape, scale, bound, pieces=(), kind=jnp.bfloat16):
    drawn = jax.random.normal(stream_key, shape, jnp.float32) * scale
    if len(pieces) > 0:
        drawn = shard_levels(stream_key, shape, pieces, -0.22, 0.18) * drawn
    return jnp.clip(drawn, min=-bound, max=bound).astype(kind)


def setup_inputs(seed: int = 0) -> dict:
    splits = jax.random.split(jax.random.key(seed), 5)
    return {
        "constraint_rows": gaussian(splits[0], (ALL_ROWS, NQ), (ALL_ROWS // 2) ** -0.5, 0.1875, ((0, 8), (1, 4)), jnp.float32),
        "shift": jnp.clip(0.3 + 0.7 * jax.random.uniform(splits[1], (NQ,), jnp.float32) ** shard_levels(splits[1], (NQ,), ((0, 4),), -0.2, 0.2), 0.3, 1.0),
        "group_rows": ragged(splits[2], N_GRP, ALL_ROWS // 2, GROUP_ROWS, 2).astype(jnp.int32),
        "panel_index": jax.random.randint(splits[3], (1,), 0, NQ // PANEL).astype(jnp.int32),
    }


def reference(constraint_rows, shift, group_rows, panel_index):
    start = panel_index[0].astype(jnp.int32) * PANEL
    rows = jnp.arange(ALL_ROWS, dtype=jnp.int32)
    counts = group_rows[rows // GROUP_ROWS]
    live = rows % GROUP_ROWS < counts
    panel_cols = lax.dynamic_slice_in_dim(constraint_rows, start, PANEL, 1)
    panel_cols = jnp.where(live[:, None], panel_cols, jnp.zeros_like(panel_cols))
    schur_panel = lax.dot_general(constraint_rows.astype(jnp.float32), panel_cols.astype(jnp.float32), (((0,), (0,)), ((), ())), precision=lax.Precision.HIGHEST, preferred_element_type=jnp.float32)
    index_rows = jnp.arange(NQ, dtype=jnp.int32)
    index_cols = jnp.arange(PANEL, dtype=jnp.int32)
    on_diag = index_rows[:, None] == start + index_cols[None, :]
    schur_panel = schur_panel + jnp.where(on_diag, shift[:, None], jnp.zeros_like(schur_panel))
    block = lax.dynamic_slice_in_dim(schur_panel, start, PANEL, 0)
    factor = jnp.linalg.cholesky(block)
    return lax.linalg.triangular_solve(factor, schur_panel, left_side=False, lower=True, transpose_a=True)
```

```python
import functools
import jax
import jax.numpy as jnp
from jax import lax
from jax.experimental import pallas as pl
from jax.experimental.pallas import tpu as pltpu
from jax.sharding import PartitionSpec as P

PANEL = 512
BLOCK = 128
LINE = 4
HIGHEST = lax.Precision.HIGHEST
HIGH = lax.Precision.HIGH


def dot(left, right, over_left, over_right, precision=HIGHEST):
    return lax.dot_general(
        left,
        right,
        (((over_left,), (over_right,)), ((), ())),
        precision=precision,
        preferred_element_type=jnp.float32,
    )


def wide(row, like):
    return jnp.broadcast_to(row, like.shape)


def eliminate(tiles, inverse):
    count = len(tiles)
    sub = lax.broadcasted_iota(jnp.int32, tiles[0].shape, 0)
    width = tiles[0].shape[1]
    done = []
    for j in range(count):
        own, inv = tiles[j], inverse[j]
        cols = [wide(own[:, 8 * j + i : 8 * j + i + 1], own) for i in range(8)]
        upper, roots, scale = {}, [], None
        for i in range(8):
            root = lax.rsqrt(wide(cols[i][i : i + 1, :], own))
            roots.append(root)
            scale = root if scale is None else jnp.where(sub >= i, root, scale)
            below = jnp.where(sub > i, cols[i] * root, 0.0)
            for m in range(i + 1, 8):
                upper[i, m] = wide(cols[m][i : i + 1, :], own) * root
                cols[m] = cols[m] - below * upper[i, m]
            own = own - below * (wide(own[i : i + 1, :], own) * root)
            inv = inv - below * (wide(inv[i : i + 1, :], own) * root)
        own, inv = own * scale, inv * scale
        done.append(inv)
        if j + 1 < count:
            nxt, nxt_inv = tiles[j + 1], inverse[j + 1]
            parts = []
            for i in range(8):
                part = wide(nxt[:, 8 * j + i : 8 * j + i + 1], own)
                for q in range(i):
                    part = part - parts[q] * upper[q, i]
                parts.append(part * roots[i])
            for i in range(8):
                nxt = nxt - parts[i] * wide(own[i : i + 1, :], own)
                nxt_inv = nxt_inv - parts[i] * wide(inv[i : i + 1, :], own)
            tiles[j + 1], inverse[j + 1] = nxt, nxt_inv
        if j + 2 < count:
            rest = dot(own, jnp.concatenate([own, inv], 1), 0, 0)
            for t in range(j + 2, count):
                tiles[t] = tiles[t] - rest[8 * t : 8 * t + 8, :width]
                inverse[t] = inverse[t] - rest[8 * t : 8 * t + 8, width:]
    return jnp.concatenate(done, 0)


def invert_step(low, first, a_in, w_in, a_ref, w_ref):
    order = a_in.shape[0]
    high = low + BLOCK
    if first:
        w_ref[...] = jnp.zeros_like(w_ref)
    else:
        w_ref[...] = w_in[...]
    lane = lax.broadcasted_iota(jnp.int32, (8, BLOCK), 1)
    sub = lax.broadcasted_iota(jnp.int32, (8, BLOCK), 0)
    steps = range(0, BLOCK, 8)
    tiles = [a_in[low + t : low + t + 8, low:high] for t in steps]
    inverse = [jnp.where(lane == sub + t, 1.0, 0.0).astype(jnp.float32) for t in steps]
    own = eliminate(tiles, inverse)
    w_ref[low:high, low:high] = own
    if low > 0:
        w_ref[low:high, :low] = dot(own, w_ref[low:high, :low], 1, 0)
    if high < order:
        below = dot(a_in[high:, low:high], own, 1, 1)
        a_ref[high:, high:] = a_in[high:, high:] - dot(below, below, 1, 1)
        w_ref[high:, :high] = w_ref[high:, :high] - dot(below, w_ref[low:high, :high], 1, 0)


def inverse_factor(block):
    order = block.shape[0]
    work, inv = block, block
    shape = jax.ShapeDtypeStruct(block.shape, jnp.float32)
    for low in range(0, order, BLOCK):
        work, inv = pl.pallas_call(
            functools.partial(invert_step, low, low == 0),
            out_shape=(shape, shape),
            compiler_params=pltpu.CompilerParams(vmem_limit_bytes=24 << 20),
            name="invert_step",
        )(work, inv)
    return inv


def add_shift(values, shift_part, first_row, start):
    row_ids = first_row + jnp.arange(values.shape[0], dtype=jnp.int32)
    col_ids = jnp.arange(values.shape[1], dtype=jnp.int32)
    on_diag = row_ids[:, None] == start + col_ids[None, :]
    return values + jnp.where(on_diag, shift_part[:, None], jnp.zeros_like(values))


def spread(value, axis, source):
    kept = jnp.where(lax.axis_index(axis) == source, value, 0).astype(value.dtype)
    return lax.psum(kept, axis)


def general(masked, local, owner, share, add_own):
    own_cols = lax.dynamic_slice_in_dim(masked, local, PANEL, 1)
    panel_cols = spread(own_cols, "col", owner)
    mine = lax.psum_scatter(dot(masked, panel_cols, 0, 0), "grp", scatter_dimension=0, tiled=True)
    mine = add_own(mine)
    from_owner = spread(mine, "col", owner)
    shard = lax.all_gather(from_owner, "grp", axis=0, tiled=True)
    block = lax.dynamic_slice_in_dim(shard, local, PANEL, 0)
    return dot(mine, inverse_factor(block), 1, 1)


def both_cores(pairs):
    return [(2 * a + core, 2 * b + core) for a, b in pairs for core in (0, 1)]


INWARD = both_cores([(0, 1), (3, 2)])
ACROSS = both_cores([(1, 2), (2, 1)])
OUTWARD = both_cores([(1, 0), (2, 3)])
SIDE = INWARD + OUTWARD


def ordered(low, mine, other, axis):
    return jnp.where(low, jnp.concatenate([mine, other], axis), jnp.concatenate([other, mine], axis))


def on_line(rows, live, shift, local, owner, start, share, add_own):
    grp, col = lax.axis_index("grp"), lax.axis_index("col")
    z, core = grp // 2, grp % 2
    left = z < 2
    core_pairs = [(g, g ^ 1) for g in range(2 * LINE)]
    x_pairs = [(c, c ^ 1) for c in range(4)]
    y_pairs = [(c, c ^ 2) for c in range(4)]

    panel = lax.dynamic_slice_in_dim(rows, local, PANEL, 1)
    panel = jnp.where((live & (col == owner))[:, None], panel, 0.0)
    diag = lax.dynamic_slice_in_dim(shift, local, PANEL, 0)
    diag = jnp.where(col == owner, diag, 0.0)
    sent = jnp.concatenate([panel, jnp.broadcast_to(diag, (8, PANEL))], 0)
    first, second = sent[:, : PANEL // 2], sent[:, PANEL // 2 :]
    first = first + lax.ppermute(first, "col", x_pairs)
    second = second + lax.ppermute(second, "col", y_pairs)
    first = first + lax.ppermute(first, "col", y_pairs)
    second = second + lax.ppermute(second, "col", x_pairs)
    sent = jnp.concatenate([first, second], 1)
    depth = rows.shape[0]
    panel, diag = sent[:depth], sent[depth]
    panel_other = lax.ppermute(panel, "grp", core_pairs)

    far_end, far_hub = jnp.where(left, 3, 0), jnp.where(left, 2, 1)

    def product(chip):
        here = lax.dynamic_slice_in_dim(rows, (2 * chip + core) * share, share, 1)
        there = lax.dynamic_slice_in_dim(rows, (2 * chip + 1 - core) * share, share, 1)
        there = lax.ppermute(there, "grp", core_pairs)
        return dot(here, panel, 0, 0, HIGH) + dot(there, panel_other, 0, 0, HIGH)

    piece = PANEL // 8
    at = (core * 4 + col) * piece
    part = dot(lax.dynamic_slice_in_dim(panel, at, piece, 1), panel, 0, 0) + dot(
        lax.dynamic_slice_in_dim(panel_other, at, piece, 1), panel_other, 0, 0
    )
    part = part + lax.ppermute(part, "grp", SIDE)
    part = part + lax.ppermute(part, "grp", ACROSS)
    outer = lax.ppermute(part, "grp", OUTWARD)
    part = jnp.where((z == 0) | (z == LINE - 1), outer, part)
    part = ordered(col % 2 == 0, part, lax.ppermute(part, "col", x_pairs), 0)
    part = ordered(col < 2, part, lax.ppermute(part, "col", y_pairs), 0)
    block = ordered(core == 0, part, lax.ppermute(part, "grp", core_pairs), 0)
    on_diag = jnp.arange(PANEL)[:, None] == jnp.arange(PANEL)[None, :]
    block = block + jnp.where(on_diag, diag[:, None], 0.0)
    inverse = inverse_factor(block)

    half = share // 2

    def halves(value):
        return [value[:half], value[half:]]

    to_end, to_hub = halves(product(far_end)), halves(product(far_hub))
    to_side, own = halves(product(z ^ 1)), halves(product(z))
    ends = [lax.ppermute(v, "grp", INWARD) for v in to_end]
    hubs = [lax.ppermute(v, "grp", INWARD) for v in to_hub]
    side = [lax.ppermute(v, "grp", INWARD) for v in to_side]
    ends = [lax.ppermute(v + r, "grp", ACROSS) for v, r in zip(to_end, ends)]
    hubs = [lax.ppermute(v + r, "grp", ACROSS) for v, r in zip(to_hub, hubs)]
    ends = [lax.ppermute(v + r, "grp", OUTWARD) for v, r in zip(to_side, ends)]
    mine = jnp.concatenate([o + e + h + s for o, e, h, s in zip(own, ends, hubs, side)], 0)
    return dot(add_own(mine), inverse, 1, 1)


def on_device(constraint_rows, shift, group_rows, panel_index):
    width = constraint_rows.shape[1]
    groups, columns = lax.axis_size("grp"), lax.axis_size("col")
    col_idx, grp_idx = lax.axis_index("col"), lax.axis_index("grp")
    share = width // groups
    start = panel_index[0] * PANEL
    owner = start // width
    local = start - owner * width
    live_count = lax.dynamic_index_in_dim(group_rows, grp_idx, keepdims=False)
    live = jnp.arange(constraint_rows.shape[0], dtype=jnp.int32) < live_count

    def add_own(mine):
        shift_part = lax.dynamic_slice_in_dim(shift, grp_idx * share, share, 0)
        return add_shift(mine, shift_part, col_idx * width + grp_idx * share, start)

    if groups == 2 * LINE and columns == 4:
        return on_line(constraint_rows, live, shift, local, owner, start, share, add_own)
    masked = jnp.where(live[:, None], constraint_rows, jnp.zeros_like(constraint_rows))
    return general(masked, local, owner, share, add_own)


def solution(mesh):
    placed = (P("grp", "col"), P("col"), P(), P())
    return jax.shard_map(
        on_device, mesh=mesh, in_specs=placed, out_specs=P(("col", "grp"), None), check_vma=False
    )
```

```python
import functools
import jax
import jax.numpy as jnp
from jax import lax
from jax.experimental import pallas as pl
from jax.experimental.pallas import tpu as pltpu
from jax.sharding import PartitionSpec as P

PANEL = 512
BLOCK = 128
LINE = 4
HIGHEST = lax.Precision.HIGHEST
HIGH = lax.Precision.HIGH


def dot(left, right, over_left, over_right, precision=HIGHEST):
    return lax.dot_general(
        left,
        right,
        (((over_left,), (over_right,)), ((), ())),
        precision=precision,
        preferred_element_type=jnp.float32,
    )


def wide(row, like):
    return jnp.broadcast_to(row, like.shape)


def eliminate(tiles, inverse):
    count = len(tiles)
    sub = lax.broadcasted_iota(jnp.int32, tiles[0].shape, 0)
    width = tiles[0].shape[1]
    done = []
    for j in range(count):
        own, inv = tiles[j], inverse[j]
        cols = [wide(own[:, 8 * j + i : 8 * j + i + 1], own) for i in range(8)]
        upper, roots, scale = {}, [], None
        for i in range(8):
            root = lax.rsqrt(wide(cols[i][i : i + 1, :], own))
            roots.append(root)
            scale = root if scale is None else jnp.where(sub >= i, root, scale)
            below = jnp.where(sub > i, cols[i] * root, 0.0)
            for m in range(i + 1, 8):
                upper[i, m] = wide(cols[m][i : i + 1, :], own) * root
                cols[m] = cols[m] - below * upper[i, m]
            own = own - below * (wide(own[i : i + 1, :], own) * root)
            inv = inv - below * (wide(inv[i : i + 1, :], own) * root)
        own, inv = own * scale, inv * scale
        done.append(inv)
        if j + 1 < count:
            nxt, nxt_inv = tiles[j + 1], inverse[j + 1]
            parts = []
            for i in range(8):
                part = wide(nxt[:, 8 * j + i : 8 * j + i + 1], own)
                for q in range(i):
                    part = part - parts[q] * upper[q, i]
                parts.append(part * roots[i])
            for i in range(8):
                nxt = nxt - parts[i] * wide(own[i : i + 1, :], own)
                nxt_inv = nxt_inv - parts[i] * wide(inv[i : i + 1, :], own)
            tiles[j + 1], inverse[j + 1] = nxt, nxt_inv
        if j + 2 < count:
            rest = dot(own, jnp.concatenate([own, inv], 1), 0, 0)
            for t in range(j + 2, count):
                tiles[t] = tiles[t] - rest[8 * t : 8 * t + 8, :width]
                inverse[t] = inverse[t] - rest[8 * t : 8 * t + 8, width:]
    return jnp.concatenate(done, 0)


def invert_step(low, first, a_in, w_in, a_ref, w_ref):
    order = a_in.shape[0]
    high = low + BLOCK
    if first:
        w_ref[...] = jnp.zeros_like(w_ref)
    else:
        w_ref[...] = w_in[...]
    lane = lax.broadcasted_iota(jnp.int32, (8, BLOCK), 1)
    sub = lax.broadcasted_iota(jnp.int32, (8, BLOCK), 0)
    steps = range(0, BLOCK, 8)
    tiles = [a_in[low + t : low + t + 8, low:high] for t in steps]
    inverse = [jnp.where(lane == sub + t, 1.0, 0.0).astype(jnp.float32) for t in steps]
    own = eliminate(tiles, inverse)
    w_ref[low:high, low:high] = own
    if low > 0:
        w_ref[low:high, :low] = dot(own, w_ref[low:high, :low], 1, 0)
    if high < order:
        below = dot(a_in[high:, low:high], own, 1, 1)
        a_ref[high:, high:] = a_in[high:, high:] - dot(below, below, 1, 1)
        w_ref[high:, :high] = w_ref[high:, :high] - dot(below, w_ref[low:high, :high], 1, 0)


def inverse_factor(block):
    order = block.shape[0]
    work, inv = block, block
    shape = jax.ShapeDtypeStruct(block.shape, jnp.float32)
    for low in range(0, order, BLOCK):
        work, inv = pl.pallas_call(
            functools.partial(invert_step, low, low == 0),
            out_shape=(shape, shape),
            compiler_params=pltpu.CompilerParams(vmem_limit_bytes=24 << 20),
            cost_estimate=pl.CostEstimate(flops=order**3, transcendentals=0, bytes_accessed=20 << 20),
            name="invert_step",
        )(work, inv)
    return inv


def add_shift(values, shift_part, first_row, start):
    row_ids = first_row + jnp.arange(values.shape[0], dtype=jnp.int32)
    col_ids = jnp.arange(values.shape[1], dtype=jnp.int32)
    on_diag = row_ids[:, None] == start + col_ids[None, :]
    return values + jnp.where(on_diag, shift_part[:, None], jnp.zeros_like(values))


def spread(value, axis, source):
    kept = jnp.where(lax.axis_index(axis) == source, value, 0).astype(value.dtype)
    return lax.psum(kept, axis)


def general(masked, local, owner, share, add_own):
    own_cols = lax.dynamic_slice_in_dim(masked, local, PANEL, 1)
    panel_cols = spread(own_cols, "col", owner)
    mine = lax.psum_scatter(dot(masked, panel_cols, 0, 0), "grp", scatter_dimension=0, tiled=True)
    mine = add_own(mine)
    from_owner = spread(mine, "col", owner)
    shard = lax.all_gather(from_owner, "grp", axis=0, tiled=True)
    block = lax.dynamic_slice_in_dim(shard, local, PANEL, 0)
    return dot(mine, inverse_factor(block), 1, 1)


def both_cores(pairs):
    return [(2 * a + core, 2 * b + core) for a, b in pairs for core in (0, 1)]


INWARD = both_cores([(0, 1), (3, 2)])
ACROSS = both_cores([(1, 2), (2, 1)])
OUTWARD = both_cores([(1, 0), (2, 3)])
SIDE = INWARD + OUTWARD


def ordered(low, mine, other, axis):
    return jnp.where(low, jnp.concatenate([mine, other], axis), jnp.concatenate([other, mine], axis))


def hold(first, second, first_in=None, second_in=None):
    if first_in is None:
        return lax.optimization_barrier((first, second))
    first, second, first_in, second_in = lax.optimization_barrier((first, second, first_in, second_in))
    return first + first_in, second + second_in


def on_line(rows, live, shift, local, owner, start, share, add_own):
    grp, col = lax.axis_index("grp"), lax.axis_index("col")
    z, core = grp // 2, grp % 2
    left = z < 2
    core_pairs = [(g, g ^ 1) for g in range(2 * LINE)]
    x_pairs = [(c, c ^ 1) for c in range(4)]
    y_pairs = [(c, c ^ 2) for c in range(4)]

    with jax.named_scope("spread"):
        panel = lax.dynamic_slice_in_dim(rows, local, PANEL, 1)
        panel = jnp.where((live & (col == owner))[:, None], panel, 0.0)
        diag = lax.dynamic_slice_in_dim(shift, local, PANEL, 0)
        diag = jnp.where(col == owner, diag, 0.0)
        sent = jnp.concatenate([panel, jnp.broadcast_to(diag, (8, PANEL))], 0)
        first, second = hold(sent[:, : PANEL // 2], sent[:, PANEL // 2 :])
        first, second = hold(
            first, second, lax.ppermute(first, "col", x_pairs), lax.ppermute(second, "col", y_pairs)
        )
        first, second = hold(first, second)
        first, second = hold(
            first, second, lax.ppermute(first, "col", y_pairs), lax.ppermute(second, "col", x_pairs)
        )
        sent = jnp.concatenate([first, second], 1)
        depth = rows.shape[0]
        panel, diag = sent[:depth], sent[depth]
        panel_other = lax.ppermute(panel, "grp", core_pairs)

    with jax.named_scope("early"):
        early = lax.dynamic_slice_in_dim(rows, 2 * (z ^ 1) * share, 2 * share, 1)
        early = lax.ppermute(early, "grp", INWARD)
        early_other = lax.dynamic_slice_in_dim(early, (1 - core) * share, share, 1)
        early_other = lax.ppermute(early_other, "grp", core_pairs)
        early = lax.dynamic_slice_in_dim(early, core * share, share, 1)
        quarter = lax.dynamic_slice_in_dim(panel, col * (depth // 4), depth // 4, 0)
        end = lax.ppermute(quarter, "grp", INWARD)
        end = ordered(col % 2 == 0, end, lax.ppermute(end, "col", x_pairs), 0)
        end = ordered(col < 2, end, lax.ppermute(end, "col", y_pairs), 0)
        end_other = lax.ppermute(end, "grp", core_pairs)

    far_end, far_hub = jnp.where(left, 3, 0), jnp.where(left, 2, 1)

    def product(chip):
        here = lax.dynamic_slice_in_dim(rows, (2 * chip + core) * share, share, 1)
        there = lax.dynamic_slice_in_dim(rows, (2 * chip + 1 - core) * share, share, 1)
        there = lax.ppermute(there, "grp", core_pairs)
        return dot(here, panel, 0, 0, HIGH) + dot(there, panel_other, 0, 0, HIGH)

    with jax.named_scope("block"):
        piece = PANEL // 8
        at = (core * 4 + col) * piece
        part = dot(lax.dynamic_slice_in_dim(panel, at, piece, 1), panel, 0, 0) + dot(
            lax.dynamic_slice_in_dim(panel_other, at, piece, 1), panel_other, 0, 0
        )
        part = part + lax.ppermute(part, "grp", SIDE)
        part = part + lax.ppermute(part, "grp", ACROSS)
        outer = lax.ppermute(part, "grp", OUTWARD)
        part = jnp.where((z == 0) | (z == LINE - 1), outer, part)
        part = ordered(col % 2 == 0, part, lax.ppermute(part, "col", x_pairs), 0)
        part = ordered(col < 2, part, lax.ppermute(part, "col", y_pairs), 0)
        block = ordered(core == 0, part, lax.ppermute(part, "grp", core_pairs), 0)
        on_diag = jnp.arange(PANEL)[:, None] == jnp.arange(PANEL)[None, :]
        block = block + jnp.where(on_diag, diag[:, None], 0.0)
    with jax.named_scope("invert"):
        inverse = inverse_factor(block)

    half = share // 2

    def halves(value):
        return [value[:half], value[half:]]

    def travel(name, values, pairs):
        out = []
        for i, value in enumerate(values):
            with jax.named_scope(f"{name}{i}"):
                out.append(lax.ppermute(value, "grp", pairs))
        return out

    to_end, to_hub = halves(product(far_end)), halves(product(far_hub))
    to_side, own = halves(product(z ^ 1)), halves(product(z))
    with jax.named_scope("early"):
        side = dot(early, end, 0, 0, HIGH) + dot(early_other, end_other, 0, 0, HIGH)
    ends = travel("in_end", to_end, INWARD)
    hubs = travel("in_hub", to_hub, INWARD)
    ends = travel("over_end", [v + r for v, r in zip(to_end, ends)], ACROSS)
    hubs = travel("over_hub", [v + r for v, r in zip(to_hub, hubs)], ACROSS)
    ends = travel("out_end", [v + r for v, r in zip(to_side, ends)], OUTWARD)
    mine = jnp.concatenate([o + e + h for o, e, h in zip(own, ends, hubs)], 0) + side
    return dot(add_own(mine), inverse, 1, 1)


def on_device(constraint_rows, shift, group_rows, panel_index):
    width = constraint_rows.shape[1]
    groups, columns = lax.axis_size("grp"), lax.axis_size("col")
    col_idx, grp_idx = lax.axis_index("col"), lax.axis_index("grp")
    share = width // groups
    start = panel_index[0] * PANEL
    owner = start // width
    local = start - owner * width
    live_count = lax.dynamic_index_in_dim(group_rows, grp_idx, keepdims=False)
    live = jnp.arange(constraint_rows.shape[0], dtype=jnp.int32) < live_count

    def add_own(mine):
        shift_part = lax.dynamic_slice_in_dim(shift, grp_idx * share, share, 0)
        return add_shift(mine, shift_part, col_idx * width + grp_idx * share, start)

    if groups == 2 * LINE and columns == 4:
        return on_line(constraint_rows, live, shift, local, owner, start, share, add_own)
    masked = jnp.where(live[:, None], constraint_rows, jnp.zeros_like(constraint_rows))
    return general(masked, local, owner, share, add_own)


def solution(mesh):
    placed = (P("grp", "col"), P("col"), P(), P())
    return jax.shard_map(
        on_device, mesh=mesh, in_specs=placed, out_specs=P(("col", "grp"), None), check_vma=False
    )
```

```python
import functools
import jax
import jax.numpy as jnp
from jax import lax
from jax.experimental import pallas as pl
from jax.experimental.pallas import tpu as pltpu
from jax.sharding import PartitionSpec as P

PANEL = 512
BLOCK = 128
LINE = 4
HIGHEST = lax.Precision.HIGHEST
HIGH = lax.Precision.HIGH


def dot(left, right, over_left, over_right, precision=HIGHEST):
    return lax.dot_general(
        left,
        right,
        (((over_left,), (over_right,)), ((), ())),
        precision=precision,
        preferred_element_type=jnp.float32,
    )


def wide(row, like):
    return jnp.broadcast_to(row, like.shape)


def eliminate(tiles, inverse):
    count = len(tiles)
    sub = lax.broadcasted_iota(jnp.int32, tiles[0].shape, 0)
    width = tiles[0].shape[1]
    done = []
    for j in range(count):
        own, inv = tiles[j], inverse[j]
        cols = [wide(own[:, 8 * j + i : 8 * j + i + 1], own) for i in range(8)]
        upper, roots, scale = {}, [], None
        for i in range(8):
            root = lax.rsqrt(wide(cols[i][i : i + 1, :], own))
            roots.append(root)
            scale = root if scale is None else jnp.where(sub >= i, root, scale)
            below = jnp.where(sub > i, cols[i] * root, 0.0)
            for m in range(i + 1, 8):
                upper[i, m] = wide(cols[m][i : i + 1, :], own) * root
                cols[m] = cols[m] - below * upper[i, m]
            own = own - below * (wide(own[i : i + 1, :], own) * root)
            inv = inv - below * (wide(inv[i : i + 1, :], own) * root)
        own, inv = own * scale, inv * scale
        done.append(inv)
        if j + 1 < count:
            nxt, nxt_inv = tiles[j + 1], inverse[j + 1]
            parts = []
            for i in range(8):
                part = wide(nxt[:, 8 * j + i : 8 * j + i + 1], own)
                for q in range(i):
                    part = part - parts[q] * upper[q, i]
                parts.append(part * roots[i])
            for i in range(8):
                nxt = nxt - parts[i] * wide(own[i : i + 1, :], own)
                nxt_inv = nxt_inv - parts[i] * wide(inv[i : i + 1, :], own)
            tiles[j + 1], inverse[j + 1] = nxt, nxt_inv
        if j + 2 < count:
            rest = dot(own, jnp.concatenate([own, inv], 1), 0, 0)
            for t in range(j + 2, count):
                tiles[t] = tiles[t] - rest[8 * t : 8 * t + 8, :width]
                inverse[t] = inverse[t] - rest[8 * t : 8 * t + 8, width:]
    return jnp.concatenate(done, 0)


def invert_step(low, first, a_in, w_in, a_ref, w_ref):
    order = a_in.shape[0]
    high = low + BLOCK
    if first:
        w_ref[...] = jnp.zeros_like(w_ref)
    else:
        w_ref[...] = w_in[...]
    lane = lax.broadcasted_iota(jnp.int32, (8, BLOCK), 1)
    sub = lax.broadcasted_iota(jnp.int32, (8, BLOCK), 0)
    steps = range(0, BLOCK, 8)
    tiles = [a_in[low + t : low + t + 8, low:high] for t in steps]
    inverse = [jnp.where(lane == sub + t, 1.0, 0.0).astype(jnp.float32) for t in steps]
    own = eliminate(tiles, inverse)
    w_ref[low:high, low:high] = own
    if low > 0:
        w_ref[low:high, :low] = dot(own, w_ref[low:high, :low], 1, 0)
    if high < order:
        below = dot(a_in[high:, low:high], own, 1, 1)
        a_ref[high:, high:] = a_in[high:, high:] - dot(below, below, 1, 1)
        w_ref[high:, :high] = w_ref[high:, :high] - dot(below, w_ref[low:high, :high], 1, 0)


def inverse_factor(block):
    order = block.shape[0]
    work, inv = block, block
    shape = jax.ShapeDtypeStruct(block.shape, jnp.float32)
    for low in range(0, order, BLOCK):
        work, inv = pl.pallas_call(
            functools.partial(invert_step, low, low == 0),
            out_shape=(shape, shape),
            compiler_params=pltpu.CompilerParams(vmem_limit_bytes=24 << 20),
            cost_estimate=pl.CostEstimate(flops=order**3, transcendentals=0, bytes_accessed=20 << 20),
            name="invert_step",
        )(work, inv)
    return inv


def add_shift(values, shift_part, first_row, start):
    row_ids = first_row + jnp.arange(values.shape[0], dtype=jnp.int32)
    col_ids = jnp.arange(values.shape[1], dtype=jnp.int32)
    on_diag = row_ids[:, None] == start + col_ids[None, :]
    return values + jnp.where(on_diag, shift_part[:, None], jnp.zeros_like(values))


def spread(value, axis, source):
    kept = jnp.where(lax.axis_index(axis) == source, value, 0).astype(value.dtype)
    return lax.psum(kept, axis)


def general(masked, local, owner, add_own):
    own_cols = lax.dynamic_slice_in_dim(masked, local, PANEL, 1)
    panel_cols = spread(own_cols, "col", owner)
    mine = lax.psum_scatter(dot(masked, panel_cols, 0, 0), "grp", scatter_dimension=0, tiled=True)
    mine = add_own(mine)
    from_owner = spread(mine, "col", owner)
    shard = lax.all_gather(from_owner, "grp", axis=0, tiled=True)
    block = lax.dynamic_slice_in_dim(shard, local, PANEL, 0)
    return dot(mine, inverse_factor(block), 1, 1)


def take_panel(index_ref, count_ref, rows_ref, shift_ref, first_ref, second_ref, held, sem):
    depth, width = held.shape[0], rows_ref.shape[1]
    start = index_ref[0] * PANEL
    owner = start // width
    local = start - owner * width
    mine = lax.axis_index("col") == owner
    limit = jnp.where(mine, count_ref[lax.axis_index("grp")], 0)
    copy = pltpu.make_async_copy(rows_ref.at[:, pl.ds(pl.multiple_of(local, PANEL), PANEL)], held, sem)
    copy.start()
    copy.wait()
    half = PANEL // 2
    live = lax.broadcasted_iota(jnp.int32, (depth, half), 0) < limit
    for side, out in enumerate((first_ref, second_ref)):
        out[:depth, :] = jnp.where(live, held[:, side * half : (side + 1) * half], 0.0)
        for q in range(half // 128):
            line = shift_ref[pl.ds(local // 128 + side * (half // 128) + q, 1), :]
            line = jnp.where(mine, line, 0.0)
            out[depth:, q * 128 : (q + 1) * 128] = jnp.broadcast_to(line, (8, 128))


def panel_halves(rows, shift, group_rows, panel_index):
    depth = rows.shape[0]
    shape = jax.ShapeDtypeStruct((depth + 8, PANEL // 2), jnp.float32)
    smem, vmem = pl.BlockSpec(memory_space=pltpu.SMEM), pl.BlockSpec(memory_space=pltpu.VMEM)
    return pl.pallas_call(
        take_panel,
        out_shape=(shape, shape),
        in_specs=[smem, smem, pl.BlockSpec(memory_space=pl.ANY), vmem],
        out_specs=(vmem, vmem),
        scratch_shapes=[pltpu.VMEM((depth, PANEL), jnp.float32), pltpu.SemaphoreType.DMA(())],
        name="take_panel",
    )(panel_index, group_rows, rows, shift.reshape(-1, 128))


def both_cores(pairs):
    return [(2 * a + core, 2 * b + core) for a, b in pairs for core in (0, 1)]


INWARD = both_cores([(0, 1), (3, 2)])
ACROSS = both_cores([(1, 2), (2, 1)])
OUTWARD = both_cores([(1, 0), (2, 3)])
SIDE = INWARD + OUTWARD


def ordered(low, mine, other, axis):
    return jnp.where(low, jnp.concatenate([mine, other], axis), jnp.concatenate([other, mine], axis))


def hold(first, second, first_in=None, second_in=None):
    if first_in is None:
        return lax.optimization_barrier((first, second))
    first, second, first_in, second_in = lax.optimization_barrier((first, second, first_in, second_in))
    return first + first_in, second + second_in


def on_line(rows, shift, group_rows, panel_index, share, add_own):
    grp, col = lax.axis_index("grp"), lax.axis_index("col")
    z, core = grp // 2, grp % 2
    left = z < 2
    core_pairs = [(g, g ^ 1) for g in range(2 * LINE)]
    x_pairs = [(c, c ^ 1) for c in range(4)]
    y_pairs = [(c, c ^ 2) for c in range(4)]

    first, second = panel_halves(rows, shift, group_rows, panel_index)
    first, second = hold(first, second, lax.ppermute(first, "col", x_pairs), lax.ppermute(second, "col", y_pairs))
    first, second = hold(first, second)
    first, second = hold(first, second, lax.ppermute(first, "col", y_pairs), lax.ppermute(second, "col", x_pairs))
    sent = jnp.concatenate([first, second], 1)
    depth = rows.shape[0]
    panel, diag = sent[:depth], sent[depth]
    panel_other = lax.ppermute(panel, "grp", core_pairs)

    early = lax.dynamic_slice_in_dim(rows, 2 * (z ^ 1) * share, 2 * share, 1)
    early = lax.ppermute(early, "grp", INWARD)
    early_other = lax.dynamic_slice_in_dim(early, (1 - core) * share, share, 1)
    early_other = lax.ppermute(early_other, "grp", core_pairs)
    early = lax.dynamic_slice_in_dim(early, core * share, share, 1)
    quarter = lax.dynamic_slice_in_dim(panel, col * (depth // 4), depth // 4, 0)
    end = lax.ppermute(quarter, "grp", INWARD)
    end = ordered(col % 2 == 0, end, lax.ppermute(end, "col", x_pairs), 0)
    end = ordered(col < 2, end, lax.ppermute(end, "col", y_pairs), 0)
    end_other = lax.ppermute(end, "grp", core_pairs)
    side = dot(early, end, 0, 0, HIGH) + dot(early_other, end_other, 0, 0, HIGH)

    piece = PANEL // 8
    at = (core * 4 + col) * piece
    part = dot(lax.dynamic_slice_in_dim(panel, at, piece, 1), panel, 0, 0) + dot(
        lax.dynamic_slice_in_dim(panel_other, at, piece, 1), panel_other, 0, 0
    )
    part = part + lax.ppermute(part, "grp", SIDE)
    part = part + lax.ppermute(part, "grp", ACROSS)
    outer = lax.ppermute(part, "grp", OUTWARD)
    part = jnp.where((z == 0) | (z == LINE - 1), outer, part)
    part = ordered(col % 2 == 0, part, lax.ppermute(part, "col", x_pairs), 0)
    part = ordered(col < 2, part, lax.ppermute(part, "col", y_pairs), 0)
    block = ordered(core == 0, part, lax.ppermute(part, "grp", core_pairs), 0)
    on_diag = jnp.arange(PANEL)[:, None] == jnp.arange(PANEL)[None, :]
    block = block + jnp.where(on_diag, diag[:, None], 0.0)
    inverse = inverse_factor(block)

    far_end, far_hub = jnp.where(left, 3, 0), jnp.where(left, 2, 1)
    to_end = [0, share // 2 - 8, share]
    to_hub = [0, share // 2 + 16, share]

    def products(chip, cuts):
        here = lax.dynamic_slice_in_dim(rows, (2 * chip + core) * share, share, 1)
        there = lax.dynamic_slice_in_dim(rows, (2 * chip + 1 - core) * share, share, 1)
        there = lax.ppermute(there, "grp", core_pairs)
        return [
            dot(here[:, lo:hi], panel, 0, 0, HIGH) + dot(there[:, lo:hi], panel_other, 0, 0, HIGH)
            for lo, hi in zip(cuts[:-1], cuts[1:])
        ]

    def travel(values, pairs):
        return [lax.ppermute(value, "grp", pairs) for value in values]

    def add(values, others):
        return [v + o for v, o in zip(values, others)]

    for_end = products(far_end, to_end)
    for_hub = products(far_hub, to_hub)
    for_side = products(z ^ 1, to_end)
    (own,) = products(z, [0, share])
    ends = travel(for_end, INWARD)
    hubs = travel(for_hub, INWARD)
    ends = travel(add(for_end, ends), ACROSS)
    hubs = travel(add(for_hub, hubs), ACROSS)
    ends = travel(add(for_side, ends), OUTWARD)
    mine = add_own(own + side) + jnp.concatenate(ends, 0) + jnp.concatenate(hubs, 0)
    return dot(mine, inverse, 1, 1)


def on_device(constraint_rows, shift, group_rows, panel_index):
    width = constraint_rows.shape[1]
    groups, columns = lax.axis_size("grp"), lax.axis_size("col")
    col_idx, grp_idx = lax.axis_index("col"), lax.axis_index("grp")
    share = width // groups
    start = panel_index[0] * PANEL
    owner = start // width
    local = start - owner * width
    live_count = lax.dynamic_index_in_dim(group_rows, grp_idx, keepdims=False)
    live = jnp.arange(constraint_rows.shape[0], dtype=jnp.int32) < live_count

    def add_own(mine):
        shift_part = lax.dynamic_slice_in_dim(shift, grp_idx * share, share, 0)
        return add_shift(mine, shift_part, col_idx * width + grp_idx * share, start)

    if groups == 2 * LINE and columns == 4:
        return on_line(constraint_rows, shift, group_rows, panel_index, share, add_own)
    masked = jnp.where(live[:, None], constraint_rows, jnp.zeros_like(constraint_rows))
    return general(masked, local, owner, add_own)


def solution(mesh):
    placed = (P("grp", "col"), P("col"), P(), P())
    return jax.shard_map(
        on_device, mesh=mesh, in_specs=placed, out_specs=P(("col", "grp"), None), check_vma=False
    )
```

```python
import functools
import jax
import jax.numpy as jnp
from jax import lax
from jax.experimental import pallas as pl
from jax.experimental.pallas import tpu as pltpu
from jax.sharding import PartitionSpec as P

PANEL = 512
BLOCK = 128
LINE = 4
HIGHEST = lax.Precision.HIGHEST


def dot(left, right, over_left, over_right, precision=HIGHEST):
    return lax.dot_general(
        left,
        right,
        (((over_left,), (over_right,)), ((), ())),
        precision=precision,
        preferred_element_type=jnp.float32,
    )


def wide(row, like):
    return jnp.broadcast_to(row, like.shape)


def eliminate(tiles, inverse):
    count = len(tiles)
    sub = lax.broadcasted_iota(jnp.int32, tiles[0].shape, 0)
    width = tiles[0].shape[1]
    done = []
    for j in range(count):
        own, inv = tiles[j], inverse[j]
        cols = [wide(own[:, 8 * j + i : 8 * j + i + 1], own) for i in range(8)]
        upper, roots, scale = {}, [], None
        for i in range(8):
            root = lax.rsqrt(wide(cols[i][i : i + 1, :], own))
            roots.append(root)
            scale = root if scale is None else jnp.where(sub >= i, root, scale)
            below = jnp.where(sub > i, cols[i] * root, 0.0)
            for m in range(i + 1, 8):
                upper[i, m] = wide(cols[m][i : i + 1, :], own) * root
                cols[m] = cols[m] - below * upper[i, m]
            own = own - below * (wide(own[i : i + 1, :], own) * root)
            inv = inv - below * (wide(inv[i : i + 1, :], own) * root)
        own, inv = own * scale, inv * scale
        done.append(inv)
        if j + 1 < count:
            nxt, nxt_inv = tiles[j + 1], inverse[j + 1]
            parts = []
            for i in range(8):
                part = wide(nxt[:, 8 * j + i : 8 * j + i + 1], own)
                for q in range(i):
                    part = part - parts[q] * upper[q, i]
                parts.append(part * roots[i])
            for i in range(8):
                nxt = nxt - parts[i] * wide(own[i : i + 1, :], own)
                nxt_inv = nxt_inv - parts[i] * wide(inv[i : i + 1, :], own)
            tiles[j + 1], inverse[j + 1] = nxt, nxt_inv
        if j + 2 < count:
            rest = dot(own, jnp.concatenate([own, inv], 1), 0, 0)
            for t in range(j + 2, count):
                tiles[t] = tiles[t] - rest[8 * t : 8 * t + 8, :width]
                inverse[t] = inverse[t] - rest[8 * t : 8 * t + 8, width:]
    return jnp.concatenate(done, 0)


def invert_step(low, first, a_in, w_in, a_ref, w_ref):
    order = a_in.shape[0]
    high = low + BLOCK
    if first:
        w_ref[...] = jnp.zeros_like(w_ref)
    else:
        w_ref[...] = w_in[...]
    lane = lax.broadcasted_iota(jnp.int32, (8, BLOCK), 1)
    sub = lax.broadcasted_iota(jnp.int32, (8, BLOCK), 0)
    steps = range(0, BLOCK, 8)
    tiles = [a_in[low + t : low + t + 8, low:high] for t in steps]
    inverse = [jnp.where(lane == sub + t, 1.0, 0.0).astype(jnp.float32) for t in steps]
    own = eliminate(tiles, inverse)
    w_ref[low:high, low:high] = own
    if low > 0:
        w_ref[low:high, :low] = dot(own, w_ref[low:high, :low], 1, 0)
    if high < order:
        below = dot(a_in[high:, low:high], own, 1, 1)
        a_ref[high:, high:] = a_in[high:, high:] - dot(below, below, 1, 1)
        w_ref[high:, :high] = w_ref[high:, :high] - dot(below, w_ref[low:high, :high], 1, 0)


def inverse_factor(block):
    order = block.shape[0]
    work, inv = block, block
    shape = jax.ShapeDtypeStruct(block.shape, jnp.float32)
    for low in range(0, order, BLOCK):
        work, inv = pl.pallas_call(
            functools.partial(invert_step, low, low == 0),
            out_shape=(shape, shape),
            compiler_params=pltpu.CompilerParams(vmem_limit_bytes=24 << 20),
            cost_estimate=pl.CostEstimate(flops=order**3, transcendentals=0, bytes_accessed=20 << 20),
            name="invert_step",
        )(work, inv)
    return inv


def add_shift(values, shift_part, first_row, start):
    row_ids = first_row + jnp.arange(values.shape[0], dtype=jnp.int32)
    col_ids = jnp.arange(values.shape[1], dtype=jnp.int32)
    on_diag = row_ids[:, None] == start + col_ids[None, :]
    return values + jnp.where(on_diag, shift_part[:, None], jnp.zeros_like(values))


def spread(value, axis, source):
    kept = jnp.where(lax.axis_index(axis) == source, value, 0).astype(value.dtype)
    return lax.psum(kept, axis)


def general(masked, local, owner, add_own):
    own_cols = lax.dynamic_slice_in_dim(masked, local, PANEL, 1)
    panel_cols = spread(own_cols, "col", owner)
    mine = lax.psum_scatter(dot(masked, panel_cols, 0, 0), "grp", scatter_dimension=0, tiled=True)
    mine = add_own(mine)
    from_owner = spread(mine, "col", owner)
    shard = lax.all_gather(from_owner, "grp", axis=0, tiled=True)
    block = lax.dynamic_slice_in_dim(shard, local, PANEL, 0)
    return dot(mine, inverse_factor(block), 1, 1)


def take_panel(index_ref, count_ref, rows_ref, shift_ref, first_ref, second_ref, side_ref, held, sem, side_sem):
    depth, width = held.shape[0], rows_ref.shape[1]
    start = index_ref[0] * PANEL
    owner = start // width
    local = start - owner * width
    mine = lax.axis_index("col") == owner
    limit = jnp.where(mine, count_ref[lax.axis_index("grp")], 0)
    copy = pltpu.make_async_copy(rows_ref.at[:, pl.ds(pl.multiple_of(local, PANEL), PANEL)], held, sem)
    copy.start()
    span = side_ref.shape[1]
    side = pl.multiple_of(((lax.axis_index("grp") // 2) ^ 1) * span, span)
    side_copy = pltpu.make_async_copy(rows_ref.at[:, pl.ds(side, span)], side_ref, side_sem)
    side_copy.start()
    copy.wait()
    half = PANEL // 2
    live = lax.broadcasted_iota(jnp.int32, (depth, half), 0) < limit
    for side, out in enumerate((first_ref, second_ref)):
        out[:depth, :] = jnp.where(live, held[:, side * half : (side + 1) * half], 0.0)
        for q in range(half // 128):
            line = shift_ref[pl.ds(local // 128 + side * (half // 128) + q, 1), :]
            line = jnp.where(mine, line, 0.0)
            out[depth:, q * 128 : (q + 1) * 128] = jnp.broadcast_to(line, (8, 128))
    side_copy.wait()


def panel_halves(rows, shift, group_rows, panel_index):
    depth = rows.shape[0]
    shape = jax.ShapeDtypeStruct((depth + 8, PANEL // 2), jnp.float32)
    smem, vmem = pl.BlockSpec(memory_space=pltpu.SMEM), pl.BlockSpec(memory_space=pltpu.VMEM)
    return pl.pallas_call(
        take_panel,
        out_shape=(shape, shape, jax.ShapeDtypeStruct((depth, rows.shape[1] // LINE), jnp.float32)),
        in_specs=[smem, smem, pl.BlockSpec(memory_space=pl.ANY), vmem],
        out_specs=(vmem, vmem, vmem),
        scratch_shapes=[pltpu.VMEM((depth, PANEL), jnp.float32)] + [pltpu.SemaphoreType.DMA(())] * 2,
        name="take_panel",
    )(panel_index, group_rows, rows, shift.reshape(-1, 128))


def both_cores(pairs):
    return [(2 * a + core, 2 * b + core) for a, b in pairs for core in (0, 1)]


INWARD = both_cores([(0, 1), (3, 2)])
ACROSS = both_cores([(1, 2), (2, 1)])
OUTWARD = both_cores([(1, 0), (2, 3)])
SIDE = INWARD + OUTWARD


def ordered(low, mine, other, axis):
    return jnp.where(low, jnp.concatenate([mine, other], axis), jnp.concatenate([other, mine], axis))


def split(value):
    high = lax.reduce_precision(value, 8, 7)
    return high.astype(jnp.bfloat16), (value - high).astype(jnp.bfloat16)


def stack_left(first, second):
    high, low = split(jnp.concatenate([first, second], 0))
    return jnp.concatenate([high, high, low], 0)


def stack_right(first, second):
    high, low = split(jnp.concatenate([first, second], 0))
    return jnp.concatenate([high, low, high], 0)


def hold(first, second, first_in=None, second_in=None):
    if first_in is None:
        return lax.optimization_barrier((first, second))
    first, second, first_in, second_in = lax.optimization_barrier((first, second, first_in, second_in))
    return first + first_in, second + second_in


def on_line(rows, shift, group_rows, panel_index, share, add_own):
    grp, col = lax.axis_index("grp"), lax.axis_index("col")
    z, core = grp // 2, grp % 2
    left = z < 2
    core_pairs = [(g, g ^ 1) for g in range(2 * LINE)]
    x_pairs = [(c, c ^ 1) for c in range(4)]
    y_pairs = [(c, c ^ 2) for c in range(4)]

    first, second, early = panel_halves(rows, shift, group_rows, panel_index)
    first, second = hold(first, second, lax.ppermute(first, "col", x_pairs), lax.ppermute(second, "col", y_pairs))
    first, second = hold(first, second)
    first, second = hold(first, second, lax.ppermute(first, "col", y_pairs), lax.ppermute(second, "col", x_pairs))
    sent = jnp.concatenate([first, second], 1)
    depth = rows.shape[0]
    panel, diag = sent[:depth], sent[depth]
    panel_other = lax.ppermute(panel, "grp", core_pairs)

    early = lax.ppermute(early, "grp", INWARD)
    early_other = lax.dynamic_slice_in_dim(early, (1 - core) * share, share, 1)
    early_other = lax.ppermute(early_other, "grp", core_pairs)
    early = lax.dynamic_slice_in_dim(early, core * share, share, 1)
    end = lax.ppermute(panel, "grp", INWARD)
    end_other = lax.ppermute(end, "grp", core_pairs)
    side = dot(stack_left(early, early_other), stack_right(end, end_other), 0, 0, None)

    piece = PANEL // 8
    at = (core * 4 + col) * piece
    part = dot(lax.dynamic_slice_in_dim(panel, at, piece, 1), panel, 0, 0) + dot(
        lax.dynamic_slice_in_dim(panel_other, at, piece, 1), panel_other, 0, 0
    )
    part = part + lax.ppermute(part, "grp", SIDE)
    part = part + lax.ppermute(part, "grp", ACROSS)
    outer = lax.ppermute(part, "grp", OUTWARD)
    part = jnp.where((z == 0) | (z == LINE - 1), outer, part)
    part = ordered(col % 2 == 0, part, lax.ppermute(part, "col", x_pairs), 0)
    part = ordered(col < 2, part, lax.ppermute(part, "col", y_pairs), 0)
    block = ordered(core == 0, part, lax.ppermute(part, "grp", core_pairs), 0)
    on_diag = jnp.arange(PANEL)[:, None] == jnp.arange(PANEL)[None, :]
    block = block + jnp.where(on_diag, diag[:, None], 0.0)
    inverse = inverse_factor(block)

    far_end, far_hub = jnp.where(left, 3, 0), jnp.where(left, 2, 1)
    to_end = [0, share // 2 - 8, share]
    to_hub = [0, share // 2 + 16, share]

    right_stack = stack_right(panel, panel_other)

    def products(chip, cuts):
        here = lax.dynamic_slice_in_dim(rows, (2 * chip + core) * share, share, 1)
        there = lax.dynamic_slice_in_dim(rows, (2 * chip + 1 - core) * share, share, 1)
        left_stack = stack_left(here, lax.ppermute(there, "grp", core_pairs))
        return [dot(left_stack[:, lo:hi], right_stack, 0, 0, None) for lo, hi in zip(cuts[:-1], cuts[1:])]

    def travel(values, pairs):
        return [lax.ppermute(value, "grp", pairs) for value in values]

    def add(values, others):
        return [v + o for v, o in zip(values, others)]

    for_end = products(far_end, to_end)
    for_hub = products(far_hub, to_hub)
    for_side = products(z ^ 1, to_end)
    (own,) = products(z, [0, share])
    ends = travel(for_end, INWARD)
    hubs = travel(for_hub, INWARD)
    ends = travel(add(for_end, ends), ACROSS)
    hubs = travel(add(for_hub, hubs), ACROSS)
    ends = travel(add(for_side, ends), OUTWARD)
    mine = add_own(own + side) + jnp.concatenate(ends, 0) + jnp.concatenate(hubs, 0)
    return dot(mine, inverse, 1, 1)


def on_device(constraint_rows, shift, group_rows, panel_index):
    width = constraint_rows.shape[1]
    groups, columns = lax.axis_size("grp"), lax.axis_size("col")
    col_idx, grp_idx = lax.axis_index("col"), lax.axis_index("grp")
    share = width // groups
    start = panel_index[0] * PANEL
    owner = start // width
    local = start - owner * width
    live_count = lax.dynamic_index_in_dim(group_rows, grp_idx, keepdims=False)
    live = jnp.arange(constraint_rows.shape[0], dtype=jnp.int32) < live_count

    def add_own(mine):
        shift_part = lax.dynamic_slice_in_dim(shift, grp_idx * share, share, 0)
        return add_shift(mine, shift_part, col_idx * width + grp_idx * share, start)

    if groups == 2 * LINE and columns == 4:
        return on_line(constraint_rows, shift, group_rows, panel_index, share, add_own)
    masked = jnp.where(live[:, None], constraint_rows, jnp.zeros_like(constraint_rows))
    return general(masked, local, owner, add_own)


def solution(mesh):
    placed = (P("grp", "col"), P("col"), P(), P())
    return jax.shard_map(
        on_device, mesh=mesh, in_specs=placed, out_specs=P(("col", "grp"), None), check_vma=False
    )
```
